256 devices in a mesh: stem: 8 (over z_lo, y), tm: 32 (over x, z_hi, core).
Axes of the slice: x: 4, y: 4, z: 8 (z_hi: 4, z_lo: 2; z = z_hi * 2 + z_lo), core: 2. Of those that a mesh axis runs over, the one named last changes fastest.
Arguments:
- frames: bfloat16 [8, 12288, 1024], P('stem', 'tm'), may hold values from -6 to 6
- timestep: int32 [8], replicated, may hold values from 0 to 49, as said below
- modulation: float32 [50, 6, 1024], replicated, may hold values from -3 to 3
- qkv_self: bfloat16 [1024, 1536], replicated, may hold values from -0.1875 to 0.1875
- out_self: bfloat16 [512, 1024], replicated, may hold values from -0.25 to 0.25
- qk_gain_self: float32 [2, 64], replicated, may hold values from 1.5 to 6
- qkv_cross: bfloat16 [1024, 1536], replicated, may hold values from -0.1875 to 0.1875
- out_cross: bfloat16 [512, 1024], replicated, may hold values from -0.25 to 0.25
- qk_gain_cross: float32 [2, 64], replicated, may hold values from 1.5 to 6
Outputs:
- layer_out: bfloat16 [8, 12288, 1024], P('stem', 'tm')
The draws below stay inside these ranges and needn't reach their ends.
Inputs may be any that keep to these rules, and one draw needn't show every extreme that they name: The stems' timestep indices are distinct, and index 0 and index 49 are always among them.
All inputs are finite; a program needn't handle non-finite values.
Results may differ from the reference program's by a relative error of at most 0.015.
The reference program's roundings to bfloat16 on the way count: a program that leaves them out, or rounds other values in their place, can miss the bound.
Values may be sent and summed in bfloat16 or wider, within the bound.
A program may use at most 128 MiB of HBM per device.

```python
import math
import jax
import jax.numpy as jnp
from jax import lax

D = 1024
H = 8
HD = 64
HW = 512
HALF = 256
STEPS = 50
STEMS = 8
FRAMES = 12288


def gain_draw(key):
    return jnp.exp(jax.random.uniform(key, (2, HD), jnp.float32, math.log(1.5), math.log(3.5)))


def draw_qk_gain_self(key, part):
    return gain_draw(jax.random.fold_in(key, 11))


def draw_qk_gain_cross(key, part):
    return gain_draw(jax.random.fold_in(key, 23))


def draw_timestep(key, part):
    inner = jax.random.permutation(jax.random.fold_in(key, 37), STEPS - 2)[:STEMS - 2].astype(jnp.int32) + 1
    ends = jnp.array([0, STEPS - 1], dtype=jnp.int32)
    values = jnp.concatenate([ends, inner])
    placing = jax.random.permutation(jax.random.fold_in(key, 41), STEMS)
    return values[placing].astype(jnp.int32)


def shard_levels(stream_key, extent, pieces, low, largest):
    loudness = 1.0
    for axis_at, shards_of in pieces:
        steps = jax.random.uniform(jax.random.fold_in(jax.random.fold_in(stream_key, 6), axis_at), (shards_of,), jnp.float32, low / len(pieces), largest / len(pieces))
        loudness = loudness * jnp.repeat(jnp.exp(steps), extent[axis_at] // shards_of).reshape((-1,) + (1,) * (len(extent) - 1 - axis_at))
    return loudness


def scatter_about(own_key, dims, scale, most, split=(), kind=jnp.bfloat16):
    level = shard_levels(own_key, dims, split, -0.22, 0.18) if split else 1.0
    values = jax.random.normal(own_key, dims, jnp.float32) * scale * level
    return jnp.minimum(jnp.maximum(values, -most), most).astype(kind)


def setup_inputs(seed: int = 0) -> dict:
    seeds = jax.random.split(jax.random.key(seed), 10)
    frames = scatter_about(seeds[0], (STEMS, FRAMES, D), 1.0, 6.0, ((0, 8), (1, 32)))
    timestep = draw_timestep(jax.random.fold_in(seeds[9], 71), 0)
    modulation = scatter_about(seeds[2], (STEPS, 6, D), 0.5, 3.0, (), jnp.float32)
    qkv_self = scatter_about(seeds[3], (D, 3 * HW), D ** -0.5, 0.1875)
    out_self = scatter_about(seeds[4], (HW, D), HW ** -0.5, 0.25)
    qk_gain_self = draw_qk_gain_self(jax.random.fold_in(seeds[9], 71), 0)
    qkv_cross = scatter_about(seeds[6], (D, 3 * HW), D ** -0.5, 0.1875)
    out_cross = scatter_about(seeds[7], (HW, D), HW ** -0.5, 0.25)
    qk_gain_cross = draw_qk_gain_cross(jax.random.fold_in(seeds[9], 71), 0)
    return {"frames": frames, "timestep": timestep, "modulation": modulation, "qkv_self": qkv_self, "out_self": out_self, "qk_gain_self": qk_gain_self, "qkv_cross": qkv_cross, "out_cross": out_cross, "qk_gain_cross": qk_gain_cross}


EPS = 1e-06
NEG = -1e+30

def rounded(values):
    return lax.optimization_barrier(values.astype(jnp.bfloat16))

def layer_norm(values):
    values = values.astype(jnp.float32)
    centred = values - lax.optimization_barrier(jnp.mean(values, axis=-1, keepdims=True))
    return centred * lax.rsqrt(lax.optimization_barrier(jnp.mean(centred * centred, axis=-1, keepdims=True)) + EPS)

def modulate(values, shift, scale):
    return layer_norm(values) * (1.0 + scale) + shift

def head_norm(values, gain):
    shaped = values.reshape(values.shape[:-1] + (H, HD))
    return shaped * lax.rsqrt(lax.optimization_barrier(jnp.mean(shaped * shaped, axis=-1, keepdims=True)) + EPS) * gain

def split_heads(projected, gains):
    width = H * HD
    query = rounded(head_norm(projected[..., :width], gains[0]))
    keyset = rounded(head_norm(projected[..., width:2 * width], gains[1]))
    valueset = rounded(projected[..., 2 * width:].reshape(projected.shape[:-1] + (H, HD)))
    return (query, keyset, valueset)

def window_stem(query, keyset, valueset):
    block = math.gcd(FRAMES, 512)
    edges = ((HALF, HALF), (0, 0), (0, 0))
    keys_pad = jnp.pad(keyset, edges)
    values_pad = jnp.pad(valueset, edges)

    def one_block(index):
        start = index * block
        q_block = lax.dynamic_slice_in_dim(query, start, block, 0).astype(jnp.float32)
        k_block = lax.dynamic_slice_in_dim(keys_pad, start, block + 2 * HALF, 0).astype(jnp.float32)
        v_block = lax.dynamic_slice_in_dim(values_pad, start, block + 2 * HALF, 0).astype(jnp.float32)
        scores = jnp.einsum('qhd,khd->hqk', q_block, k_block) * HD ** (-0.5)
        q_pos = start + jnp.arange(block, dtype=jnp.int32)
        k_pos = start - HALF + jnp.arange(block + 2 * HALF, dtype=jnp.int32)
        keep = (jnp.abs(q_pos[:, None] - k_pos[None, :]) <= HALF) & (k_pos[None, :] >= 0) & (k_pos[None, :] < FRAMES)
        scores = jnp.where(keep[None], scores, NEG)
        weights = rounded(jax.nn.softmax(scores, axis=-1)).astype(jnp.float32)
        return jnp.einsum('hqk,khd->qhd', weights, v_block)
    blocks = lax.map(one_block, jnp.arange(FRAMES // block, dtype=jnp.int32))
    return rounded(blocks.reshape(FRAMES, H * HD))

def reference(frames, timestep, modulation, qkv_self, out_self, qk_gain_self, qkv_cross, out_cross, qk_gain_cross):
    width = H * HD
    modulations = modulation[timestep][:, :, None, :]
    normed_self = rounded(modulate(frames, modulations[:, 0], modulations[:, 1]))
    projected = jnp.dot(normed_self.reshape(-1, D), qkv_self, preferred_element_type=jnp.float32).reshape(STEMS, FRAMES, 3 * width)
    query, keyset, valueset = split_heads(projected, qk_gain_self)
    attended = lax.map(lambda packed: window_stem(packed[0], packed[1], packed[2]), (query, keyset, valueset))
    mixed = jnp.dot(attended.reshape(-1, width), out_self, preferred_element_type=jnp.float32).reshape(STEMS, FRAMES, D)
    first = rounded(frames.astype(jnp.float32) + modulations[:, 2] * mixed)
    normed_cross = rounded(modulate(first, modulations[:, 3], modulations[:, 4]))
    projected_cross = jnp.dot(normed_cross.reshape(-1, D), qkv_cross, preferred_element_type=jnp.float32).reshape(STEMS, FRAMES, 3 * width)
    q_cross, k_cross, v_cross = split_heads(projected_cross, qk_gain_cross)
    scores = jnp.einsum('sfhd,tfhd->fhst', q_cross.astype(jnp.float32), k_cross.astype(jnp.float32)) * HD ** (-0.5)
    weights = rounded(jax.nn.softmax(scores, axis=-1)).astype(jnp.float32)
    attended_cross = rounded(jnp.einsum('fhst,tfhd->sfhd', weights, v_cross.astype(jnp.float32))).reshape(STEMS * FRAMES, width)
    cross_out = rounded(jnp.dot(attended_cross, out_cross, preferred_element_type=jnp.float32)).reshape(STEMS, FRAMES, D)
    return (first.astype(jnp.float32) + modulations[:, 5] * cross_out.astype(jnp.float32)).astype(jnp.bfloat16)
```

```python
import jax
import jax.numpy as jnp
from jax import lax
from jax.experimental import pallas as pl
from jax.experimental.pallas import tpu as pltpu
from jax.sharding import PartitionSpec as P

HD = 64
EPS = 1e-06
NEG = -1e30
BLK = 128
F32 = jnp.float32
BF16 = jnp.bfloat16
MESH = pl.DeviceIdType.MESH


def matmul(a, b):
    return jnp.dot(a, b, preferred_element_type=F32)


def matmul_nt(a, b):
    return lax.dot_general(a, b, (((1,), (1,)), ((), ())), preferred_element_type=F32)


def make_kernel(stems, tms, steps, rows, width, hw):
    blocks = rows // BLK
    part = BLK // stems
    pairs = hw // 128

    def kernel(
        frames_hbm, timestep_hbm, mod_hbm, w1_hbm, wo1_hbm, g1_hbm, w2_hbm, wo2_hbm, g2_hbm,
        out_hbm,
        x_buf, t_smem, mod_buf, w1, wo1, g1, w2, wo2, g2, gains, diag,
        norm_buf, q_buf, kv_buf, m_buf, o_buf, attn_buf,
        first_buf, recv_buf, cmix_buf, recv2_buf, out_buf,
        load_sem, store_sem, hs_sem, hr_sem, as_sem, ar_sem, bs_sem, br_sem,
    ):
        me_s = lax.axis_index("stem")
        me_t = lax.axis_index("tm")
        left, right = me_t - 1, me_t + 1
        half = stems // 2
        me_hi, me_lo = me_s // half, lax.rem(me_s, half)
        peers = [
            lax.rem(me_hi + r // half, 2) * half + lax.rem(me_lo + r % half, half)
            for r in range(stems)
        ]
        order = list(range(half, stems)) + list(range(1, half))
        has_left, has_right = me_t > 0, me_t < tms - 1

        loads = [
            pltpu.make_async_copy(src, dst, load_sem.at[i])
            for i, (src, dst) in enumerate([
                (timestep_hbm, t_smem), (frames_hbm, x_buf.at[pl.ds(2 * BLK, rows), :]),
                (mod_hbm, mod_buf), (w1_hbm, w1),
                (g1_hbm, g1), (g2_hbm, g2), (wo1_hbm, wo1), (w2_hbm, w2), (wo2_hbm, wo2),
            ])
        ]
        barrier = pltpu.get_barrier_semaphore()

        def greet(to):
            pl.semaphore_signal(barrier, inc=1, device_id=to, device_id_type=MESH)

        for r in order:
            greet({"stem": peers[r]})

        @pl.when(has_left)
        def _():
            greet({"tm": left})

        @pl.when(has_right)
        def _():
            greet({"tm": right})

        for load in loads:
            load.start()

        def halo_copy(index, source_block, target_block, to):
            return pltpu.make_async_remote_copy(
                src_ref=frames_hbm.at[pl.ds(source_block * BLK, BLK), :],
                dst_ref=x_buf.at[pl.ds(target_block * BLK, BLK), :],
                send_sem=hs_sem.at[index],
                recv_sem=hr_sem.at[index],
                device_id={"tm": to},
                device_id_type=MESH,
            )

        to_left = [halo_copy(0, 0, 5, left), halo_copy(2, 1, 6, left)]
        to_right = [halo_copy(1, 2, 1, right), halo_copy(3, 1, 0, right)]

        pl.semaphore_wait(
            barrier, stems - 1 + has_left.astype(jnp.int32) + has_right.astype(jnp.int32)
        )
        for step in range(2):
            pl.when(has_left)(to_left[step].start)
            pl.when(has_right)(to_right[step].start)

        @pl.when(jnp.logical_not(has_left))
        def _():
            x_buf[0 : 2 * BLK, :] = jnp.zeros((2 * BLK, width), BF16)

        @pl.when(jnp.logical_not(has_right))
        def _():
            x_buf[rows + 2 * BLK :, :] = jnp.zeros((2 * BLK, width), BF16)

        def halo_arrived(step):
            pl.when(has_right)(to_left[step].wait_recv)
            pl.when(has_left)(to_right[step].wait_recv)

        row = lax.broadcasted_iota(jnp.int32, (256, 256), 0)
        col = lax.broadcasted_iota(jnp.int32, (256, 256), 1)
        diag[...] = jnp.where((row >> 6) == (col >> 6), 1.0 / HD, 0.0).astype(BF16)

        loads[4].wait()
        loads[5].wait()
        for i, g in enumerate((g1, g2)):
            two = jnp.concatenate([g[...], g[...]], axis=1)
            wide = jnp.concatenate([two] * pairs, axis=1)
            gains[2 * i : 2 * i + 1, :] = wide[0:1] * (HD ** -0.5)
            gains[2 * i + 1 : 2 * i + 2, :] = wide[1:2]

        def normed(values, shift, scale):
            values = values.astype(F32)
            centred = values - jnp.mean(values, axis=-1, keepdims=True)
            var = jnp.mean(centred * centred, axis=-1, keepdims=True)
            return (centred * lax.rsqrt(var + EPS) * scale + shift).astype(BF16)

        def head_norm(values, gain):
            square = (values * values).astype(BF16)
            mean = jnp.concatenate(
                [matmul(square[:, i : i + 256], diag[...]) for i in range(0, hw, 256)], axis=1
            )
            return (values * lax.rsqrt(mean + EPS) * gain).astype(BF16)

        loads[0].wait()
        loads[1].wait()
        loads[2].wait()
        t_own = t_smem[me_s]

        def mods(which, at):
            return mod_buf[which, pl.ds(at, 1), :]

        shift1, scale1 = mods(0, t_own), mods(1, t_own) + 1.0

        def norm_rows(i, carry):
            at = pl.ds(pl.multiple_of(i * 32, 32), 32)
            norm_buf[at, :] = normed(x_buf[at, :], shift1, scale1)
            return carry

        def norm_blocks(first, last):
            lax.fori_loop(first * (BLK // 32), last * (BLK // 32), norm_rows, 0)

        def key_values(block):
            at = pl.ds(block * BLK, BLK)
            keys = matmul(norm_buf[at, :], w1[:, hw : 2 * hw])
            kv_buf[0, at, :] = head_norm(keys, gains[1:2, :])
            kv_buf[1, at, :] = matmul(norm_buf[at, :], w1[:, 2 * hw :]).astype(BF16)

        norm_blocks(2, 5)
        loads[3].wait()
        for block in (2, 3, 4):
            key_values(block)
        for block in range(blocks):
            at = pl.ds((2 + block) * BLK, BLK)
            q_buf[pl.ds(block * BLK, BLK), :] = head_norm(
                matmul(norm_buf[at, :], w1[:, :hw]), gains[0:1, :]
            )

        r_at = lax.broadcasted_iota(jnp.int32, (2 * BLK, BLK), 0) & (BLK - 1)
        c_at = lax.broadcasted_iota(jnp.int32, (2 * BLK, BLK), 1)
        low_lanes = lax.broadcasted_iota(jnp.int32, (BLK, 128), 1) < HD
        bias_left = jnp.where(me_t == 0, NEG, 0.0).astype(F32)
        bias_right = jnp.where(me_t == tms - 1, NEG, 0.0).astype(F32)

        def two_heads(q):
            zero = jnp.zeros_like(q)
            return jnp.concatenate(
                [jnp.where(low_lanes, q, zero), jnp.where(low_lanes, zero, q)], axis=0
            )

        def with_ones(v):
            return jnp.concatenate([v, jnp.ones_like(v)], axis=1)

        def keep(scores, kind):
            if kind == -1:
                return jnp.where(c_at >= r_at, scores, NEG)
            if kind == 1:
                return jnp.where(c_at <= r_at, scores, NEG)
            return scores

        def pieces(block, pair, spans):
            lanes = pl.ds(pair * 128, 128)
            q2 = two_heads(q_buf[pl.ds(block * BLK, BLK), lanes])
            scores, values = [], []
            for start, kind, bias in spans:
                at = pl.ds(start * BLK, BLK)
                part_scores = matmul_nt(q2, kv_buf[0, at, lanes])
                if bias is not None:
                    part_scores = part_scores + bias
                scores.append(keep(part_scores, kind))
                values.append(with_ones(kv_buf[1, at, lanes]))
            return jnp.concatenate(scores, axis=1), jnp.concatenate(values, axis=0)

        own_spans = {
            0: [(2, 0, None), (3, 0, None), (4, 1, None)],
            1: [(2, 0, None), (3, 0, None), (4, 0, None)],
            2: [(2, -1, None), (3, 0, None), (4, 0, None)],
        }
        halo_spans = {
            0: [(0, -1, bias_left), (1, 0, bias_left)],
            1: [(1, -1, bias_left), (5, 1, bias_right)],
            2: [(5, 0, bias_right), (6, 1, bias_right)],
        }

        def own_part(block):
            for pair in range(pairs):
                scores, values = pieces(block, pair, own_spans[block])
                top = jnp.max(scores, axis=-1, keepdims=True)
                raised = jnp.exp(scores - top).astype(BF16)
                m_buf[block, pair] = jnp.broadcast_to(top, (2 * BLK, 128))
                o_buf[block, pair] = matmul(raised, values)

        def halo_part(block):
            for pair in range(pairs):
                scores, values = pieces(block, pair, halo_spans[block])
                before = m_buf[block, pair][:, 0:1]
                top = jnp.maximum(before, jnp.max(scores, axis=-1, keepdims=True))
                raised = jnp.exp(scores - top).astype(BF16)
                total = o_buf[block, pair] * jnp.exp(before - top) + matmul(raised, values)
                mixed = total[:, :128] / total[:, 128:]
                both = jnp.where(low_lanes, mixed[:BLK], mixed[BLK:])
                attn_buf[:, pl.ds(pair * 128, 128)] = both.astype(BF16)

        gate1 = mods(2, t_own)

        def first_copy(block, r):
            return pltpu.make_async_remote_copy(
                src_ref=first_buf.at[block, peers[r]],
                dst_ref=recv_buf.at[block, me_s],
                send_sem=as_sem.at[block, r],
                recv_sem=ar_sem.at[block, r],
                device_id={"stem": peers[r]},
                device_id_type=MESH,
            )

        def home_copy(block, r):
            return pltpu.make_async_remote_copy(
                src_ref=cmix_buf.at[block, peers[r]],
                dst_ref=recv2_buf.at[block, me_s],
                send_sem=bs_sem.at[block, r],
                recv_sem=br_sem.at[block, r],
                device_id={"stem": peers[r]},
                device_id_type=MESH,
            )

        def first_part(block):
            at = pl.ds((2 + block) * BLK, BLK)
            value = x_buf[at, :].astype(F32) + gate1 * matmul(attn_buf[...], wo1[...])
            first_buf[block] = value.astype(BF16).reshape(stems, part, width)
            recv_buf[block, me_s] = first_buf[block, me_s]
            for r in order:
                first_copy(block, r).start()

        def cross_part(block):
            for r in order:
                first_copy(block, r).wait_recv()
            for s in range(stems):
                norm_buf[s * part : (s + 1) * part, :] = normed(
                    recv_buf[block, s], mods(3, t_smem[s]), mods(4, t_smem[s]) + 1.0
                )
            rows_in = norm_buf[0:BLK, :]
            q = head_norm(matmul(rows_in, w2[:, :hw]), gains[2:3, :])
            k = head_norm(matmul(rows_in, w2[:, hw : 2 * hw]), gains[3:4, :])
            v = matmul(rows_in, w2[:, 2 * hw :]).astype(BF16)
            same = (r_at & (part - 1)) == (c_at & (part - 1))
            for pair in range(pairs):
                lanes = slice(pair * 128, pair * 128 + 128)
                scores = jnp.where(same, matmul_nt(two_heads(q[:, lanes]), k[:, lanes]), NEG)
                top = jnp.max(scores, axis=-1, keepdims=True)
                raised = jnp.exp(scores - top).astype(BF16)
                total = matmul(raised, with_ones(v[:, lanes]))
                mixed = total[:, :128] / total[:, 128:]
                both = jnp.where(low_lanes, mixed[:BLK], mixed[BLK:]).astype(BF16)
                cmix_buf[block, :, :, lanes] = both.reshape(stems, part, 128)
            recv2_buf[block, me_s] = cmix_buf[block, me_s]
            for r in order:
                home_copy(block, r).start()

        gate2 = mods(5, t_own)

        def last_part(block):
            for r in order:
                home_copy(block, r).wait_recv()
            cross = matmul(recv2_buf[block].reshape(BLK, hw), wo2[...]).astype(BF16).astype(F32)
            first = first_buf[block].reshape(BLK, width).astype(F32)
            out_buf[pl.ds(block * BLK, BLK), :] = (first + gate2 * cross).astype(BF16)
            store(block).start()

        def store(block):
            at = pl.ds(block * BLK, BLK)
            return pltpu.make_async_copy(out_buf.at[at, :], out_hbm.at[at, :], store_sem.at[block])

        for block in (1, 0, 2):
            own_part(block)
        loads[6].wait()
        halo_arrived(0)
        for block in (1, 5):
            norm_blocks(block, block + 1)
            key_values(block)
        halo_part(1)
        first_part(1)
        halo_arrived(1)
        for block, halo in ((0, 0), (2, 6)):
            norm_blocks(halo, halo + 1)
            key_values(halo)
            halo_part(block)
            first_part(block)
        loads[7].wait()
        for block in (1, 0, 2):
            cross_part(block)
        loads[8].wait()
        for block in (1, 0, 2):
            last_part(block)

        for step in range(2):
            pl.when(has_left)(to_left[step].wait_send)
            pl.when(has_right)(to_right[step].wait_send)
        for block in (1, 0, 2):
            for r in order:
                first_copy(block, r).wait_send()
                home_copy(block, r).wait_send()
            store(block).wait()

    return kernel


def solution(mesh):
    stems, tms = mesh.shape["stem"], mesh.shape["tm"]

    def on_device(
        frames, timestep, modulation, qkv_self, out_self, gain_self, qkv_cross, out_cross, gain_cross
    ):
        rows, width = frames.shape[1:]
        hw = out_self.shape[0]
        steps = modulation.shape[0]
        blocks, part, pairs = rows // BLK, BLK // stems, hw // 128
        result = pl.pallas_call(
            make_kernel(stems, tms, steps, rows, width, hw),
            out_shape=jax.ShapeDtypeStruct((rows, width), BF16),
            in_specs=[pl.BlockSpec(memory_space=pl.ANY)] * 9,
            out_specs=pl.BlockSpec(memory_space=pl.ANY),
            scratch_shapes=[
                pltpu.VMEM((rows + 4 * BLK, width), BF16),
                pltpu.SMEM((stems,), jnp.int32),
                pltpu.VMEM((6, steps, width), F32),
                pltpu.VMEM((width, 3 * hw), BF16),
                pltpu.VMEM((hw, width), BF16),
                pltpu.VMEM((2, HD), F32),
                pltpu.VMEM((width, 3 * hw), BF16),
                pltpu.VMEM((hw, width), BF16),
                pltpu.VMEM((2, HD), F32),
                pltpu.VMEM((4, hw), F32),
                pltpu.VMEM((256, 256), BF16),
                pltpu.VMEM((rows + 4 * BLK, width), BF16),
                pltpu.VMEM((rows, hw), BF16),
                pltpu.VMEM((2, rows + 4 * BLK, hw), BF16),
                pltpu.VMEM((blocks, pairs, 2 * BLK, 128), F32),
                pltpu.VMEM((blocks, pairs, 2 * BLK, 256), F32),
                pltpu.VMEM((BLK, hw), BF16),
                pltpu.VMEM((blocks, stems, part, width), BF16),
                pltpu.VMEM((blocks, stems, part, width), BF16),
                pltpu.VMEM((blocks, stems, part, hw), BF16),
                pltpu.VMEM((blocks, stems, part, hw), BF16),
                pltpu.VMEM((rows, width), BF16),
                pltpu.SemaphoreType.DMA((9,)),
                pltpu.SemaphoreType.DMA((blocks,)),
                pltpu.SemaphoreType.DMA((4,)),
                pltpu.SemaphoreType.DMA((4,)),
                pltpu.SemaphoreType.DMA((blocks, stems)),
                pltpu.SemaphoreType.DMA((blocks, stems)),
                pltpu.SemaphoreType.DMA((blocks, stems)),
                pltpu.SemaphoreType.DMA((blocks, stems)),
            ],
            compiler_params=pltpu.CompilerParams(
                collective_id=0, has_side_effects=True, vmem_limit_bytes=60 << 20
            ),
            name="block",
        )(
            frames.reshape(rows, width), timestep, modulation.transpose(1, 0, 2), qkv_self, out_self, gain_self,
            qkv_cross, out_cross, gain_cross,
        )
        return result[None]

    return jax.shard_map(
        on_device,
        mesh=mesh,
        in_specs=(P("stem", "tm", None), P(), P(), P(), P(), P(), P(), P(), P()),
        out_specs=P("stem", "tm", None),
        check_vma=False,
    )
```

```python
import jax
import jax.numpy as jnp
from jax import lax
from jax.experimental import pallas as pl
from jax.experimental.pallas import tpu as pltpu
from jax.sharding import PartitionSpec as P

HD = 64
EPS = 1e-06
NEG = -1e30
BLK = 128
F32 = jnp.float32
BF16 = jnp.bfloat16
MESH = pl.DeviceIdType.MESH


def matmul(a, b):
    return jnp.dot(a, b, preferred_element_type=F32)


def matmul_nt(a, b):
    return lax.dot_general(a, b, (((1,), (1,)), ((), ())), preferred_element_type=F32)


def make_kernel(stems, tms, steps, rows, width, hw):
    blocks = rows // BLK
    part = BLK // stems
    pairs = hw // 128

    def kernel(
        frames_hbm, timestep_hbm, mod_hbm, w1_hbm, wo1_hbm, g1_hbm, w2_hbm, wo2_hbm, g2_hbm,
        out_hbm,
        x_buf, t_smem, mod_buf, w1, wo1, g1, w2, wo2, g2, gains, diag,
        norm_buf, q_buf, kv_buf, m_buf, o_buf, e_buf, attn_buf, back_buf, got_buf, back_lse, got_lse,
        first_buf, recv_buf, cmix_buf, recv2_buf, out_buf,
        load_sem, store_sem, hs_sem, hr_sem, as_sem, ar_sem, bs_sem, br_sem,
    ):
        me_s = lax.axis_index("stem")
        me_t = lax.axis_index("tm")
        odd = lax.rem(me_t, 2)
        beyond, partner = me_t - 1 + 2 * odd, me_t + 1 - 2 * odd
        has_beyond = jnp.logical_and(beyond >= 0, beyond < tms)

        def rows_of(block):
            place = block + odd * (blocks - 1 - 2 * block)
            return pl.ds(pl.multiple_of(place * BLK, BLK), BLK)

        half = stems // 2
        me_hi, me_lo = me_s // half, lax.rem(me_s, half)
        peers = [
            lax.rem(me_hi + r // half, 2) * half + lax.rem(me_lo + r % half, half)
            for r in range(stems)
        ]
        order = list(range(half, stems)) + list(range(1, half))

        loads = [
            pltpu.make_async_copy(src, dst, load_sem.at[i])
            for i, (src, dst) in enumerate([
                (timestep_hbm, t_smem), (mod_hbm, mod_buf), (g1_hbm, g1), (g2_hbm, g2),
                (w1_hbm, w1), (wo1_hbm, wo1), (w2_hbm, w2), (wo2_hbm, wo2),
            ])
        ]
        barrier = pltpu.get_barrier_semaphore()

        def greet(to):
            pl.semaphore_signal(barrier, inc=1, device_id=to, device_id_type=MESH)

        for r in order:
            greet({"stem": peers[r]})

        greet({"tm": partner})

        @pl.when(has_beyond)
        def _():
            greet({"tm": beyond})

        own_loads = [
            pltpu.make_async_copy(
                frames_hbm.at[rows_of(block), :],
                x_buf.at[pl.ds((2 + block) * BLK, BLK), :],
                load_sem.at[8 + block],
            )
            for block in range(blocks)
        ]
        loads[0].start()
        for load in own_loads:
            load.start()
        for load in loads[1:]:
            load.start()

        def near_copy(index, block, slot, to):
            return pltpu.make_async_remote_copy(
                src_ref=frames_hbm.at[rows_of(block), :],
                dst_ref=x_buf.at[pl.ds(slot * BLK, BLK), :],
                send_sem=hs_sem.at[index],
                recv_sem=hr_sem.at[index],
                device_id={"tm": to},
                device_id_type=MESH,
            )

        def far_copy(index, slot, to):
            return pltpu.make_async_remote_copy(
                src_ref=kv_buf.at[:, pl.ds(3 * BLK, BLK), :],
                dst_ref=kv_buf.at[:, pl.ds(slot * BLK, BLK), :],
                send_sem=hs_sem.at[index],
                recv_sem=hr_sem.at[index],
                device_id={"tm": to},
                device_id_type=MESH,
            )

        near_beyond = near_copy(0, 0, 1, beyond)
        near_partner = near_copy(1, 2, 5, partner)
        far_partner = far_copy(2, 6, partner)
        backs = [
            pltpu.make_async_remote_copy(
                src_ref=source,
                dst_ref=target,
                send_sem=hs_sem.at[index],
                recv_sem=hr_sem.at[index],
                device_id={"tm": beyond},
                device_id_type=MESH,
            )
            for index, source, target in ((3, back_buf, got_buf), (4, back_lse, got_lse))
        ]

        pl.semaphore_wait(barrier, stems + has_beyond.astype(jnp.int32))
        pl.when(has_beyond)(near_beyond.start)
        near_partner.start()

        @pl.when(jnp.logical_not(has_beyond))
        def _():
            x_buf[BLK : 2 * BLK, :] = jnp.zeros((BLK, width), BF16)
            got_buf[...] = jnp.zeros((BLK, hw), BF16)
            got_lse[...] = jnp.full((8, BLK), NEG, F32)

        row = lax.broadcasted_iota(jnp.int32, (256, 256), 0)
        col = lax.broadcasted_iota(jnp.int32, (256, 256), 1)
        diag[...] = jnp.where((row >> 6) == (col >> 6), 1.0 / HD, 0.0).astype(BF16)

        loads[2].wait()
        loads[3].wait()
        for i, g in enumerate((g1, g2)):
            two = jnp.concatenate([g[...], g[...]], axis=1)
            wide = jnp.concatenate([two] * pairs, axis=1)
            gains[2 * i : 2 * i + 1, :] = wide[0:1] * (HD ** -0.5)
            gains[2 * i + 1 : 2 * i + 2, :] = wide[1:2]

        def normed(values, shift, scale):
            values = values.astype(F32)
            centred = values - jnp.mean(values, axis=-1, keepdims=True)
            var = jnp.mean(centred * centred, axis=-1, keepdims=True)
            return (centred * lax.rsqrt(var + EPS) * scale + shift).astype(BF16)

        def head_norm(values, gain):
            square = (values * values).astype(BF16)
            mean = jnp.concatenate(
                [matmul(square[:, i : i + 256], diag[...]) for i in range(0, hw, 256)], axis=1
            )
            return (values * lax.rsqrt(mean + EPS) * gain).astype(BF16)

        loads[0].wait()
        loads[1].wait()
        t_own = t_smem[me_s]

        def mods(which, at):
            return mod_buf[which, pl.ds(at, 1), :]

        shift1, scale1 = mods(0, t_own), mods(1, t_own) + 1.0

        def norm_blocks(first, last):
            def one(block, carry):
                for i in range(BLK // 16):
                    at = pl.ds(pl.multiple_of(block * BLK + i * 16, 16), 16)
                    norm_buf[at, :] = normed(x_buf[at, :], shift1, scale1)
                return carry

            lax.fori_loop(first, last, one, 0)

        def key_values(block):
            at = pl.ds(block * BLK, BLK)
            keys = matmul(norm_buf[at, :], w1[:, hw : 2 * hw])
            kv_buf[0, at, :] = head_norm(keys, gains[1:2, :])
            kv_buf[1, at, :] = matmul(norm_buf[at, :], w1[:, 2 * hw :]).astype(BF16)

        for load in own_loads:
            load.wait()
        norm_blocks(2, 5)
        loads[4].wait()
        key_values(3)
        key_values(2)
        far_partner.start()
        key_values(4)

        def queries(block):
            at = pl.ds((2 + block) * BLK, BLK)
            q_buf[pl.ds((1 + block) * BLK, BLK), :] = head_norm(
                matmul(norm_buf[at, :], w1[:, :hw]), gains[0:1, :]
            )

        for block in range(blocks):
            queries(block)

        r_at = lax.broadcasted_iota(jnp.int32, (2 * BLK, BLK), 0) & (BLK - 1)
        c_at = lax.broadcasted_iota(jnp.int32, (2 * BLK, BLK), 1)
        low_lanes = lax.broadcasted_iota(jnp.int32, (BLK, 128), 1) < HD
        bias = jnp.where(has_beyond, 0.0, NEG).astype(F32)
        slope = (c_at - r_at) * (1 - 2 * odd)

        def two_heads(q):
            zero = jnp.zeros_like(q)
            return jnp.concatenate(
                [jnp.where(low_lanes, q, zero), jnp.where(low_lanes, zero, q)], axis=0
            )

        def with_ones(v):
            return jnp.concatenate([v, jnp.ones_like(v)], axis=1)

        def pieces(block, pair, first, last):
            lanes = pl.ds(pair * 128, 128)
            at = pl.ds(first * BLK, (last - first) * BLK)
            q2 = two_heads(q_buf[pl.ds((1 + block) * BLK, BLK), lanes])
            scores = matmul_nt(q2, kv_buf[0, at, lanes])
            parts = []
            for slot in range(first, last):
                piece = scores[:, (slot - first) * BLK : (slot - first + 1) * BLK]
                if slot == block:
                    piece = jnp.where(slope >= 0, piece, NEG)
                if slot == block + 4:
                    piece = jnp.where(slope <= 0, piece, NEG)
                if slot < 2:
                    piece = piece + bias
                parts.append(piece)
            return jnp.concatenate(parts, axis=1), with_ones(kv_buf[1, at, lanes])

        lane = lax.broadcasted_iota(jnp.int32, (BLK, 128), 1)

        def heads(values):
            return jnp.where(low_lanes, values[:BLK], values[BLK:])

        def finish(pair, total, into):
            mixed = total[:, :128] / total[:, 128:]
            into[:, pl.ds(pair * 128, 128)] = heads(mixed).astype(BF16)

        def attend(block, first, last):
            for pair in range(pairs):
                scores, values = pieces(block, pair, first, last)
                top = jnp.max(scores, axis=-1, keepdims=True)
                total = matmul(jnp.exp(scores - top).astype(BF16), values)
                if block == 2:
                    finish(pair, total, attn_buf)
                elif block == 1:
                    m_buf[pair] = jnp.broadcast_to(top, (2 * BLK, 128))
                    o_buf[pair] = total
                else:
                    e_buf[pair, 0] = heads(jnp.broadcast_to(top, (2 * BLK, 128)))
                    e_buf[pair, 1] = heads(total[:, :128])
                    e_buf[pair, 2] = heads(total[:, 128:])

        def attend_more():
            for pair in range(pairs):
                scores, values = pieces(1, pair, 1, 2)
                before = m_buf[pair][:, 0:1]
                top = jnp.maximum(before, jnp.max(scores, axis=-1, keepdims=True))
                total = matmul(jnp.exp(scores - top).astype(BF16), values)
                finish(pair, total + o_buf[pair] * jnp.exp(before - top), attn_buf)

        def attend_back():
            stats = jnp.zeros((BLK, 128), F32)
            for pair in range(pairs):
                scores, values = pieces(-1, pair, 3, 4)
                top = jnp.max(scores, axis=-1, keepdims=True)
                total = matmul(jnp.exp(scores - top).astype(BF16), values)
                finish(pair, total, back_buf)
                lse = top + jnp.log(total[:, 128:])
                stats = jnp.where(lane == 2 * pair, lse[:BLK], stats)
                stats = jnp.where(lane == 2 * pair + 1, lse[BLK:], stats)
            back_lse[...] = jnp.transpose(stats)[:8, :]

        def attend_got():
            filler = jnp.zeros((BLK - 8, BLK), F32)
            stats = jnp.transpose(jnp.concatenate([got_lse[...], filler], axis=0))
            for pair in range(pairs):
                lanes = pl.ds(pair * 128, 128)
                lse = jnp.where(
                    low_lanes, stats[:, 2 * pair : 2 * pair + 1], stats[:, 2 * pair + 1 : 2 * pair + 2]
                )
                before = e_buf[pair, 0]
                top = jnp.maximum(before, lse)
                own, other = jnp.exp(before - top), jnp.exp(lse - top)
                mixed = e_buf[pair, 1] * own + got_buf[:, lanes].astype(F32) * other
                attn_buf[:, lanes] = (mixed / (e_buf[pair, 2] * own + other)).astype(BF16)

        gate1 = mods(2, t_own)

        def first_copy(block, r):
            return pltpu.make_async_remote_copy(
                src_ref=first_buf.at[block, peers[r]],
                dst_ref=recv_buf.at[block, me_s],
                send_sem=as_sem.at[block, r],
                recv_sem=ar_sem.at[block, r],
                device_id={"stem": peers[r]},
                device_id_type=MESH,
            )

        def home_copy(block, r):
            return pltpu.make_async_remote_copy(
                src_ref=cmix_buf.at[block, peers[r]],
                dst_ref=recv2_buf.at[block, me_s],
                send_sem=bs_sem.at[block, r],
                recv_sem=br_sem.at[block, r],
                device_id={"stem": peers[r]},
                device_id_type=MESH,
            )

        def first_part(block):
            at = pl.ds((2 + block) * BLK, BLK)
            value = x_buf[at, :].astype(F32) + gate1 * matmul(attn_buf[...], wo1[...])
            first_buf[block] = value.astype(BF16).reshape(stems, part, width)
            recv_buf[block, me_s] = first_buf[block, me_s]
            for r in order:
                first_copy(block, r).start()

        def cross_part(block):
            for r in order:
                first_copy(block, r).wait_recv()
            for s in range(stems):
                norm_buf[s * part : (s + 1) * part, :] = normed(
                    recv_buf[block, s], mods(3, t_smem[s]), mods(4, t_smem[s]) + 1.0
                )
            rows_in = norm_buf[0:BLK, :]
            q = head_norm(matmul(rows_in, w2[:, :hw]), gains[2:3, :])
            k = head_norm(matmul(rows_in, w2[:, hw : 2 * hw]), gains[3:4, :])
            v = matmul(rows_in, w2[:, 2 * hw :]).astype(BF16)
            same = (r_at & (part - 1)) == (c_at & (part - 1))
            for pair in range(pairs):
                lanes = slice(pair * 128, pair * 128 + 128)
                scores = jnp.where(same, matmul_nt(two_heads(q[:, lanes]), k[:, lanes]), NEG)
                top = jnp.max(scores, axis=-1, keepdims=True)
                raised = jnp.exp(scores - top).astype(BF16)
                total = matmul(raised, with_ones(v[:, lanes]))
                mixed = total[:, :128] / total[:, 128:]
                both = jnp.where(low_lanes, mixed[:BLK], mixed[BLK:]).astype(BF16)
                cmix_buf[block, :, :, lanes] = both.reshape(stems, part, 128)
            recv2_buf[block, me_s] = cmix_buf[block, me_s]

        def send_home(block):
            for r in order:
                home_copy(block, r).start()

        gate2 = mods(5, t_own)

        def last_part(block):
            for r in order:
                home_copy(block, r).wait_recv()
            cross = matmul(recv2_buf[block].reshape(BLK, hw), wo2[...]).astype(BF16).astype(F32)
            first = first_buf[block].reshape(BLK, width).astype(F32)
            out_buf[pl.ds(block * BLK, BLK), :] = (first + gate2 * cross).astype(BF16)
            store(block).start()

        def store(block):
            at = pl.ds(block * BLK, BLK)
            return pltpu.make_async_copy(
                out_buf.at[at, :], out_hbm.at[rows_of(block), :], store_sem.at[block]
            )

        near_partner.wait_recv()
        norm_blocks(5, 6)
        key_values(5)
        far_partner.wait_recv()
        attend(2, 2, 7)
        loads[5].wait()
        first_part(2)
        attend(1, 2, 6)
        pl.when(has_beyond)(near_beyond.wait_recv)
        norm_blocks(1, 2)
        queries(-1)
        attend_back()
        key_values(1)
        for back in backs:
            pl.when(has_beyond)(back.start)
        attend_more()
        first_part(1)
        attend(0, 1, 5)
        loads[6].wait()
        cross_part(2)
        for back in backs:
            pl.when(has_beyond)(back.wait_recv)
        attend_got()
        first_part(0)
        send_home(2)
        cross_part(1)
        send_home(1)
        loads[7].wait()
        last_part(2)
        cross_part(0)
        send_home(0)
        last_part(1)
        last_part(0)

        pl.when(has_beyond)(near_beyond.wait_send)
        for back in backs:
            pl.when(has_beyond)(back.wait_send)
        near_partner.wait_send()
        far_partner.wait_send()
        for block in (1, 0, 2):
            for r in order:
                first_copy(block, r).wait_send()
                home_copy(block, r).wait_send()
            store(block).wait()

    return kernel


def solution(mesh):
    stems, tms = mesh.shape["stem"], mesh.shape["tm"]

    def on_device(
        frames, timestep, modulation, qkv_self, out_self, gain_self, qkv_cross, out_cross, gain_cross
    ):
        rows, width = frames.shape[1:]
        hw = out_self.shape[0]
        steps = modulation.shape[0]
        blocks, part, pairs = rows // BLK, BLK // stems, hw // 128
        result = pl.pallas_call(
            make_kernel(stems, tms, steps, rows, width, hw),
            out_shape=jax.ShapeDtypeStruct((rows, width), BF16),
            in_specs=[pl.BlockSpec(memory_space=pltpu.HBM)] * 9,
            out_specs=pl.BlockSpec(memory_space=pl.ANY),
            scratch_shapes=[
                pltpu.VMEM((rows + 4 * BLK, width), BF16),
                pltpu.SMEM((stems,), jnp.int32),
                pltpu.VMEM((6, steps, width), F32),
                pltpu.VMEM((width, 3 * hw), BF16),
                pltpu.VMEM((hw, width), BF16),
                pltpu.VMEM((2, HD), F32),
                pltpu.VMEM((width, 3 * hw), BF16),
                pltpu.VMEM((hw, width), BF16),
                pltpu.VMEM((2, HD), F32),
                pltpu.VMEM((4, hw), F32),
                pltpu.VMEM((256, 256), BF16),
                pltpu.VMEM((rows + 4 * BLK, width), BF16),
                pltpu.VMEM((rows + BLK, hw), BF16),
                pltpu.VMEM((2, rows + 4 * BLK, hw), BF16),
                pltpu.VMEM((pairs, 2 * BLK, 128), F32),
                pltpu.VMEM((pairs, 2 * BLK, 256), F32),
                pltpu.VMEM((pairs, 3, BLK, 128), F32),
                pltpu.VMEM((BLK, hw), BF16),
                pltpu.VMEM((BLK, hw), BF16),
                pltpu.VMEM((BLK, hw), BF16),
                pltpu.VMEM((8, BLK), F32),
                pltpu.VMEM((8, BLK), F32),
                pltpu.VMEM((blocks, stems, part, width), BF16),
                pltpu.VMEM((blocks, stems, part, width), BF16),
                pltpu.VMEM((blocks, stems, part, hw), BF16),
                pltpu.VMEM((blocks, stems, part, hw), BF16),
                pltpu.VMEM((rows, width), BF16),
                pltpu.SemaphoreType.DMA((8 + blocks,)),
                pltpu.SemaphoreType.DMA((blocks,)),
                pltpu.SemaphoreType.DMA((5,)),
                pltpu.SemaphoreType.DMA((5,)),
                pltpu.SemaphoreType.DMA((blocks, stems)),
                pltpu.SemaphoreType.DMA((blocks, stems)),
                pltpu.SemaphoreType.DMA((blocks, stems)),
                pltpu.SemaphoreType.DMA((blocks, stems)),
            ],
            compiler_params=pltpu.CompilerParams(
                collective_id=0, has_side_effects=True, vmem_limit_bytes=36 << 20
            ),
            name="block",
        )(
            *(
                pltpu.with_memory_space_constraint(value, pltpu.HBM)
                for value in (
                    frames.reshape(rows, width), timestep, modulation.transpose(1, 0, 2),
                    qkv_self, out_self, gain_self, qkv_cross, out_cross, gain_cross,
                )
            )
        )
        return result[None]

    return jax.shard_map(
        on_device,
        mesh=mesh,
        in_specs=(P("stem", "tm", None), P(), P(), P(), P(), P(), P(), P(), P()),
        out_specs=P("stem", "tm", None),
        check_vma=False,
    )
```

```python
import jax
import jax.numpy as jnp
from jax import lax
from jax.experimental import pallas as pl
from jax.experimental.pallas import tpu as pltpu
from jax.sharding import PartitionSpec as P

HD = 64
EPS = 1e-06
NEG = -1e30
BLK = 128
F32 = jnp.float32
BF16 = jnp.bfloat16
MESH = pl.DeviceIdType.MESH


def matmul(a, b):
    return jnp.dot(a, b, preferred_element_type=F32)


def matmul_nt(a, b):
    return lax.dot_general(a, b, (((1,), (1,)), ((), ())), preferred_element_type=F32)


def make_kernel(stems, tms, steps, rows, width, hw):
    blocks = rows // BLK
    part = BLK // stems
    pairs = hw // 128

    def kernel(
        frames_hbm, timestep_hbm, mod_hbm, w1_hbm, wo1_hbm, g1_hbm, w2_hbm, wo2_hbm, g2_hbm,
        out_ref,
        x_buf, t_smem, mod_buf, w1, wo1, g1, w2, wo2, g2, gains, diag,
        norm_buf, q_buf, kv_buf, m_buf, o_buf, e_buf, attn_buf, back_buf, got_buf, back_lse, got_lse,
        first_buf, recv_buf, cmix_buf, recv2_buf,
        load_sem, hs_sem, hr_sem, as_sem, ar_sem, bs_sem, br_sem,
    ):
        me_s = lax.axis_index("stem")
        me_t = lax.axis_index("tm")
        odd = lax.rem(me_t, 2)
        beyond, partner = me_t - 1 + 2 * odd, me_t + 1 - 2 * odd
        has_beyond = jnp.logical_and(beyond >= 0, beyond < tms)

        def rows_of(block):
            place = block + odd * (blocks - 1 - 2 * block)
            return pl.ds(pl.multiple_of(place * BLK, BLK), BLK)

        half, fold = stems // 2, BLK // 2

        def chunk_of(stem):
            hi, lo = stem // half, lax.rem(stem, half)
            return half * (1 - lo // 2) + 2 * hi + lax.rem(lo, 2)

        me_hi, me_lo = me_s // half, lax.rem(me_s, half)

        def shifted(r, sign):
            hi = lax.rem(me_hi + r // half, 2)
            return hi * half + lax.rem(me_lo + half + sign * (r % half), half)

        peers = [shifted(r, 1) for r in range(stems)]
        sources = [shifted(r, -1) for r in range(stems)]
        near_side, far_side = [2, 1, 3], [6, 5, 7, 4]
        order = far_side + near_side

        def others(action, which=None):
            for r in order:
                if which is None:
                    action(r)
                else:
                    in_first = lax.rem(peers[r], half) < half // 2
                    pl.when(in_first == (which == 1))(lambda r=r: action(r))

        loads = [
            pltpu.make_async_copy(src, dst, load_sem.at[i])
            for i, (src, dst) in enumerate([
                (timestep_hbm, t_smem), (mod_hbm, mod_buf), (g1_hbm, g1), (g2_hbm, g2),
                (w1_hbm, w1), (wo1_hbm, wo1), (w2_hbm, w2), (wo2_hbm, wo2),
            ])
        ]
        barrier = pltpu.get_barrier_semaphore()

        def greet(to):
            pl.semaphore_signal(barrier, inc=1, device_id=to, device_id_type=MESH)

        others(lambda r: greet({"stem": peers[r]}))
        greet({"tm": partner})

        @pl.when(has_beyond)
        def _():
            greet({"tm": beyond})

        own_loads = [
            pltpu.make_async_copy(
                frames_hbm.at[rows_of(block), :],
                x_buf.at[pl.ds((2 + block) * BLK, BLK), :],
                load_sem.at[8 + block],
            )
            for block in range(blocks)
        ]
        loads[0].start()
        for load in own_loads:
            load.start()
        for load in loads[1:]:
            load.start()

        def near_copy(index, block, slot, to, skip=0, size=BLK):
            place = block + odd * (blocks - 1 - 2 * block)
            return pltpu.make_async_remote_copy(
                src_ref=frames_hbm.at[pl.ds(pl.multiple_of(place * BLK + skip, 16), size), :],
                dst_ref=x_buf.at[pl.ds(slot * BLK + skip, size), :],
                send_sem=hs_sem.at[index],
                recv_sem=hr_sem.at[index],
                device_id={"tm": to},
                device_id_type=MESH,
            )

        def far_copy(index, slot, to):
            return pltpu.make_async_remote_copy(
                src_ref=kv_buf.at[:, pl.ds(3 * BLK, BLK), :],
                dst_ref=kv_buf.at[:, pl.ds(slot * BLK, BLK), :],
                send_sem=hs_sem.at[index],
                recv_sem=hr_sem.at[index],
                device_id={"tm": to},
                device_id_type=MESH,
            )

        near_beyond = [near_copy(h, 0, 1, beyond, h * fold, fold) for h in range(2)]
        near_partner = near_copy(2, 2, 5, partner)
        far_partner = far_copy(3, 6, partner)
        backs = [
            [
                pltpu.make_async_remote_copy(
                    src_ref=source,
                    dst_ref=target,
                    send_sem=hs_sem.at[index],
                    recv_sem=hr_sem.at[index],
                    device_id={"tm": beyond},
                    device_id_type=MESH,
                )
                for index, source, target in (
                    (4 + h, back_buf.at[pl.ds(h * fold, fold), :], got_buf.at[pl.ds(h * fold, fold), :]),
                    (6 + h, back_lse.at[h], got_lse.at[h]),
                )
            ]
            for h in range(2)
        ]

        pl.semaphore_wait(barrier, stems + has_beyond.astype(jnp.int32))
        pl.when(has_beyond)(near_beyond[1].start)
        pl.when(has_beyond)(near_beyond[0].start)
        near_partner.start()

        @pl.when(jnp.logical_not(has_beyond))
        def _():
            x_buf[BLK : 2 * BLK, :] = jnp.zeros((BLK, width), BF16)
            got_buf[...] = jnp.zeros((BLK, hw), BF16)
            got_lse[...] = jnp.full((2, 8, BLK), NEG, F32)

        row = lax.broadcasted_iota(jnp.int32, (256, 256), 0)
        col = lax.broadcasted_iota(jnp.int32, (256, 256), 1)
        diag[...] = jnp.where((row >> 6) == (col >> 6), 1.0 / HD, 0.0).astype(BF16)

        loads[2].wait()
        loads[3].wait()
        for i, g in enumerate((g1, g2)):
            two = jnp.concatenate([g[...], g[...]], axis=1)
            wide = jnp.concatenate([two] * pairs, axis=1)
            gains[2 * i : 2 * i + 1, :] = wide[0:1] * (HD ** -0.5)
            gains[2 * i + 1 : 2 * i + 2, :] = wide[1:2]

        def normed(values, shift, scale):
            values = values.astype(F32)
            centred = values - jnp.mean(values, axis=-1, keepdims=True)
            var = jnp.mean(centred * centred, axis=-1, keepdims=True)
            return (centred * lax.rsqrt(var + EPS) * scale + shift).astype(BF16)

        def head_norm(values, gain):
            square = (values * values).astype(BF16)
            mean = jnp.concatenate(
                [matmul(square[:, i : i + 256], diag[...]) for i in range(0, hw, 256)], axis=1
            )
            return (values * lax.rsqrt(mean + EPS) * gain).astype(BF16)

        loads[0].wait()
        loads[1].wait()
        t_own = t_smem[me_s]

        def mods(which, at):
            return mod_buf[which, pl.ds(at, 1), :]

        shift1, scale1 = mods(0, t_own), mods(1, t_own) + 1.0

        def norm_blocks(first, last):
            def one(block, carry):
                for i in range(BLK // 16):
                    at = pl.ds(pl.multiple_of(block * BLK + i * 16, 16), 16)
                    norm_buf[at, :] = normed(x_buf[at, :], shift1, scale1)
                return carry

            lax.fori_loop(first, last, one, 0)

        def norm_half(h):
            for i in range(fold // 16):
                at = pl.ds(BLK + h * fold + i * 16, 16)
                norm_buf[at, :] = normed(x_buf[at, :], shift1, scale1)

        def key_values(block):
            at = pl.ds(block * BLK, BLK)
            keys = matmul(norm_buf[at, :], w1[:, hw : 2 * hw])
            kv_buf[0, at, :] = head_norm(keys, gains[1:2, :])
            kv_buf[1, at, :] = matmul(norm_buf[at, :], w1[:, 2 * hw :]).astype(BF16)

        for load in own_loads:
            load.wait()
        norm_blocks(2, 5)
        loads[4].wait()
        key_values(3)
        key_values(2)
        far_partner.start()
        key_values(4)

        def queries(block):
            at = pl.ds((2 + block) * BLK, BLK)
            q_buf[pl.ds((1 + block) * BLK, BLK), :] = head_norm(
                matmul(norm_buf[at, :], w1[:, :hw]), gains[0:1, :]
            )

        def queries_half(h):
            q_buf[pl.ds(h * fold, fold), :] = head_norm(
                matmul(norm_buf[pl.ds(BLK + h * fold, fold), :], w1[:, :hw]), gains[0:1, :]
            )

        for block in range(blocks):
            queries(block)

        r_at = lax.broadcasted_iota(jnp.int32, (2 * BLK, BLK), 0) & (BLK - 1)
        c_at = lax.broadcasted_iota(jnp.int32, (2 * BLK, BLK), 1)
        low_lanes = lax.broadcasted_iota(jnp.int32, (BLK, 128), 1) < HD
        bias = jnp.where(has_beyond, 0.0, NEG).astype(F32)
        slope = (c_at - r_at) * (1 - 2 * odd)

        def two_heads(q):
            zero, low = jnp.zeros_like(q), low_lanes[: q.shape[0]]
            return jnp.concatenate([jnp.where(low, q, zero), jnp.where(low, zero, q)], axis=0)

        def with_ones(v):
            return jnp.concatenate([v, jnp.ones_like(v)], axis=1)

        def pieces(block, pair, first, last):
            lanes = pl.ds(pair * 128, 128)
            at = pl.ds(first * BLK, (last - first) * BLK)
            q2 = two_heads(q_buf[pl.ds((1 + block) * BLK, BLK), lanes])
            scores = matmul_nt(q2, kv_buf[0, at, lanes])
            parts = []
            for slot in range(first, last):
                piece = scores[:, (slot - first) * BLK : (slot - first + 1) * BLK]
                if slot == block:
                    piece = jnp.where(slope >= 0, piece, NEG)
                if slot == block + 4:
                    piece = jnp.where(slope <= 0, piece, NEG)
                if slot < 2:
                    piece = piece + bias
                parts.append(piece)
            return jnp.concatenate(parts, axis=1), with_ones(kv_buf[1, at, lanes])

        lane = lax.broadcasted_iota(jnp.int32, (BLK, 128), 1)

        def heads(values):
            n = values.shape[0] // 2
            return jnp.where(low_lanes[:n], values[:n], values[n:])

        def finish(pair, total, into, rows_at=slice(None)):
            mixed = total[:, :128] / total[:, 128:]
            into[rows_at, pl.ds(pair * 128, 128)] = heads(mixed).astype(BF16)

        def attend(block, first, last):
            for pair in range(pairs):
                scores, values = pieces(block, pair, first, last)
                top = jnp.max(scores, axis=-1, keepdims=True)
                total = matmul(jnp.exp(scores - top).astype(BF16), values)
                if block == 2:
                    finish(pair, total, attn_buf)
                elif block == 1:
                    m_buf[pair] = jnp.broadcast_to(top, (2 * BLK, 128))
                    o_buf[pair] = total
                else:
                    e_buf[pair, 0] = heads(jnp.broadcast_to(top, (2 * BLK, 128)))
                    e_buf[pair, 1] = heads(total[:, :128])
                    e_buf[pair, 2] = heads(total[:, 128:])

        def attend_more():
            for pair in range(pairs):
                scores, values = pieces(1, pair, 1, 2)
                before = m_buf[pair][:, 0:1]
                top = jnp.maximum(before, jnp.max(scores, axis=-1, keepdims=True))
                total = matmul(jnp.exp(scores - top).astype(BF16), values)
                finish(pair, total + o_buf[pair] * jnp.exp(before - top), attn_buf)

        def attend_back(h):
            stats = jnp.zeros((fold, 128), F32)
            at, keys = pl.ds(h * fold, fold), pl.ds(3 * BLK, BLK)
            r_half = (lax.broadcasted_iota(jnp.int32, (BLK, BLK), 0) & (fold - 1)) + h * fold
            tilt = (c_at[:BLK] - r_half) * (1 - 2 * odd)
            for pair in range(pairs):
                lanes = pl.ds(pair * 128, 128)
                scores = matmul_nt(two_heads(q_buf[at, lanes]), kv_buf[0, keys, lanes])
                scores = jnp.where(tilt <= 0, scores, NEG)
                top = jnp.max(scores, axis=-1, keepdims=True)
                total = matmul(jnp.exp(scores - top).astype(BF16), with_ones(kv_buf[1, keys, lanes]))
                finish(pair, total, back_buf, at)
                lse = top + jnp.log(total[:, 128:])
                stats = jnp.where(lane[:fold] == 2 * pair, lse[:fold], stats)
                stats = jnp.where(lane[:fold] == 2 * pair + 1, lse[fold:], stats)
            filler = jnp.zeros((BLK - fold, 128), F32)
            back_lse[h] = jnp.transpose(jnp.concatenate([stats, filler], axis=0))[:8, :]

        def attend_got(h):
            at = pl.ds(h * fold, fold)
            filler = jnp.zeros((BLK - 8, BLK), F32)
            stats = jnp.transpose(jnp.concatenate([got_lse[h], filler], axis=0))[:fold]
            for pair in range(pairs):
                lanes = pl.ds(pair * 128, 128)
                lse = jnp.where(
                    low_lanes[:fold],
                    stats[:, 2 * pair : 2 * pair + 1],
                    stats[:, 2 * pair + 1 : 2 * pair + 2],
                )
                before = e_buf[pair, 0, at, :]
                top = jnp.maximum(before, lse)
                own, other = jnp.exp(before - top), jnp.exp(lse - top)
                mixed = e_buf[pair, 1, at, :] * own + got_buf[at, lanes].astype(F32) * other
                attn_buf[at, lanes] = (mixed / (e_buf[pair, 2, at, :] * own + other)).astype(BF16)

        gate1 = mods(2, t_own)

        def first_copy(block, r, source):
            return pltpu.make_async_remote_copy(
                src_ref=first_buf.at[block, chunk_of(peers[r])],
                dst_ref=recv_buf.at[block, source],
                send_sem=as_sem.at[block, r],
                recv_sem=ar_sem.at[block, r],
                device_id={"stem": peers[r]},
                device_id_type=MESH,
            )

        def home_copy(block, r, source):
            return pltpu.make_async_remote_copy(
                src_ref=cmix_buf.at[block, peers[r]],
                dst_ref=recv2_buf.at[block, chunk_of(source)],
                send_sem=bs_sem.at[block, r],
                recv_sem=br_sem.at[block, r],
                device_id={"stem": peers[r]},
                device_id_type=MESH,
            )

        def first_part(block, skip=0, size=BLK):
            at = pl.ds((2 + block) * BLK + skip, size)
            value = x_buf[at, :].astype(F32) + gate1 * matmul(attn_buf[pl.ds(skip, size), :], wo1[...])
            first_buf[block, pl.ds(skip // part, size // part)] = value.astype(BF16).reshape(
                size // part, part, width
            )

        def send_first(block, which=None):
            others(lambda r: first_copy(block, r, me_s).start(), which)

        def keep_first(block):
            recv_buf[block, me_s] = first_buf[block, chunk_of(me_s)]

        def cross_part(block):
            for group in ([0] + near_side, far_side):
                for r in group:
                    if r:
                        first_copy(block, r, sources[r]).wait_recv()
                for r in group:
                    s = sources[r]
                    at = pl.ds(pl.multiple_of(s * part, part), part)
                    norm_buf[at, :] = normed(
                        recv_buf[block, s], mods(3, t_smem[s]), mods(4, t_smem[s]) + 1.0
                    )
            rows_in = norm_buf[0:BLK, :]
            q = head_norm(matmul(rows_in, w2[:, :hw]), gains[2:3, :])
            k = head_norm(matmul(rows_in, w2[:, hw : 2 * hw]), gains[3:4, :])
            v = matmul(rows_in, w2[:, 2 * hw :]).astype(BF16)
            same = (r_at & (part - 1)) == (c_at & (part - 1))
            for pair in range(pairs):
                lanes = slice(pair * 128, pair * 128 + 128)
                scores = jnp.where(same, matmul_nt(two_heads(q[:, lanes]), k[:, lanes]), NEG)
                top = jnp.max(scores, axis=-1, keepdims=True)
                raised = jnp.exp(scores - top).astype(BF16)
                total = matmul(raised, with_ones(v[:, lanes]))
                mixed = total[:, :128] / total[:, 128:]
                both = jnp.where(low_lanes, mixed[:BLK], mixed[BLK:]).astype(BF16)
                cmix_buf[block, :, :, lanes] = both.reshape(stems, part, 128)
            recv2_buf[block, chunk_of(me_s)] = cmix_buf[block, me_s]

        def send_home(block):
            others(lambda r: home_copy(block, r, me_s).start())

        gate2 = mods(5, t_own)

        def last_part(block):
            others(lambda r: home_copy(block, r, sources[r]).wait_recv())
            cross = matmul(recv2_buf[block].reshape(BLK, hw), wo2[...]).astype(BF16).astype(F32)
            first = first_buf[block].reshape(BLK, width).astype(F32)
            out_ref[rows_of(block), :] = (first + gate2 * cross).astype(BF16)

        near_partner.wait_recv()
        norm_blocks(5, 6)
        key_values(5)
        far_partner.wait_recv()
        attend(2, 2, 7)
        loads[5].wait()
        first_part(2)
        send_first(2)
        keep_first(2)
        for h in (1, 0):
            pl.when(has_beyond)(near_beyond[h].wait_recv)
            norm_half(h)
            queries_half(h)
            attend_back(h)
            for back in backs[h]:
                pl.when(has_beyond)(back.start)
            if h:
                attend(1, 2, 6)
        key_values(1)
        attend_more()
        first_part(1)
        send_first(1)
        keep_first(1)
        attend(0, 1, 5)
        loads[6].wait()
        for h in (1, 0):
            for back in backs[h]:
                pl.when(has_beyond)(back.wait_recv)
            attend_got(h)
            first_part(0, h * fold, fold)
            send_first(0, h)
        keep_first(0)
        cross_part(2)
        send_home(2)
        cross_part(1)
        send_home(1)
        loads[7].wait()
        cross_part(0)
        send_home(0)
        last_part(2)
        last_part(1)
        last_part(0)

        for copy in near_beyond + backs[0] + backs[1]:
            pl.when(has_beyond)(copy.wait_send)
        near_partner.wait_send()
        far_partner.wait_send()
        for block in (1, 0, 2):
            others(lambda r: first_copy(block, r, me_s).wait_send())
            others(lambda r: home_copy(block, r, me_s).wait_send())

    return kernel


def solution(mesh):
    stems, tms = mesh.shape["stem"], mesh.shape["tm"]

    def on_device(
        frames, timestep, modulation, qkv_self, out_self, gain_self, qkv_cross, out_cross, gain_cross
    ):
        rows, width = frames.shape[1:]
        hw = out_self.shape[0]
        steps = modulation.shape[0]
        blocks, part, pairs = rows // BLK, BLK // stems, hw // 128
        result = pl.pallas_call(
            make_kernel(stems, tms, steps, rows, width, hw),
            out_shape=jax.ShapeDtypeStruct((rows, width), BF16),
            in_specs=[pl.BlockSpec(memory_space=pltpu.HBM)] * 9,
            out_specs=pl.BlockSpec(memory_space=pltpu.VMEM),
            scratch_shapes=[
                pltpu.VMEM((rows + 4 * BLK, width), BF16),
                pltpu.SMEM((stems,), jnp.int32),
                pltpu.VMEM((6, steps, width), F32),
                pltpu.VMEM((width, 3 * hw), BF16),
                pltpu.VMEM((hw, width), BF16),
                pltpu.VMEM((2, HD), F32),
                pltpu.VMEM((width, 3 * hw), BF16),
                pltpu.VMEM((hw, width), BF16),
                pltpu.VMEM((2, HD), F32),
                pltpu.VMEM((4, hw), F32),
                pltpu.VMEM((256, 256), BF16),
                pltpu.VMEM((rows + 4 * BLK, width), BF16),
                pltpu.VMEM((rows + BLK, hw), BF16),
                pltpu.VMEM((2, rows + 4 * BLK, hw), BF16),
                pltpu.VMEM((pairs, 2 * BLK, 128), F32),
                pltpu.VMEM((pairs, 2 * BLK, 256), F32),
                pltpu.VMEM((pairs, 3, BLK, 128), F32),
                pltpu.VMEM((BLK, hw), BF16),
                pltpu.VMEM((BLK, hw), BF16),
                pltpu.VMEM((BLK, hw), BF16),
                pltpu.VMEM((2, 8, BLK), F32),
                pltpu.VMEM((2, 8, BLK), F32),
                pltpu.VMEM((blocks, stems, part, width), BF16),
                pltpu.VMEM((blocks, stems, part, width), BF16),
                pltpu.VMEM((blocks, stems, part, hw), BF16),
                pltpu.VMEM((blocks, stems, part, hw), BF16),
                pltpu.SemaphoreType.DMA((8 + blocks,)),
                pltpu.SemaphoreType.DMA((8,)),
                pltpu.SemaphoreType.DMA((8,)),
                pltpu.SemaphoreType.DMA((blocks, stems)),
                pltpu.SemaphoreType.DMA((blocks, stems)),
                pltpu.SemaphoreType.DMA((blocks, stems)),
                pltpu.SemaphoreType.DMA((blocks, stems)),
            ],
            compiler_params=pltpu.CompilerParams(
                collective_id=0, has_side_effects=True, vmem_limit_bytes=36 << 20
            ),
            name="block",
        )(
            *(
                pltpu.with_memory_space_constraint(value, pltpu.HBM)
                for value in (
                    frames.reshape(rows, width), timestep, modulation.transpose(1, 0, 2),
                    qkv_self, out_self, gain_self, qkv_cross, out_cross, gain_cross,
                )
            )
        )
        return result[None]

    return jax.shard_map(
        on_device,
        mesh=mesh,
        in_specs=(P("stem", "tm", None), P(), P(), P(), P(), P(), P(), P(), P()),
        out_specs=P("stem", "tm", None),
        check_vma=False,
    )
```
